32 devices in a mesh: dp: 8 (over y, x, core), mp: 4 (over z).
Axes of the slice: x: 2, y: 2, z: 4, core: 2. Of those that a mesh axis runs over, the one named last changes fastest.
Arguments:
- tokens: bfloat16 [16384, 768], P(('dp', 'mp')), may hold values from -6 to 6
- doc_ids: int32 [32, 512], P('dp'), may hold values from 0 to 7, never falling along the last dimension, each value on 1 to 192 neighbouring positions
- w_qkv: bfloat16 [3, 768, 768], P(None, None, 'mp'), may hold values from -0.21875 to 0.21875
- bias_qv: bfloat16 [2, 768], P(None, 'mp'), may hold values from -3 to 3
- w_out: bfloat16 [768, 768], P('mp'), may hold values from -1.75 to 1.75
- bias_out: bfloat16 [768], replicated, may hold values from -2 to 2
- gain_attn: bfloat16 [768], replicated, may hold values from 0.5 to 1.5
- shift_attn: bfloat16 [768], replicated, may hold values from -2 to 2
- w_up: bfloat16 [768, 3072], P(None, 'mp'), may hold values from -0.21875 to 0.21875
- bias_up: bfloat16 [3072], P('mp'), may hold values from -3 to 3
- w_down: bfloat16 [3072, 768], P('mp'), may hold values from -0.109375 to 0.109375
- bias_down: bfloat16 [768], replicated, may hold values from -2 to 2
- gain_mlp: bfloat16 [768], replicated, may hold values from 0.5 to 1.5
- shift_mlp: bfloat16 [768], replicated, may hold values from -2 to 2
- out_grad: bfloat16 [16384, 768], P(('dp', 'mp')), may hold values from -6 to 6
Outputs:
- layer_out: bfloat16 [16384, 768], P(('dp', 'mp'))
- grad_tokens: bfloat16 [16384, 768], P(('dp', 'mp'))
- grad_w_qkv: float32 [3, 768, 768], P(None, None, 'mp')
- grad_bias_qv: float32 [2, 768], P(None, 'mp')
- grad_w_out: float32 [768, 768], P('mp')
- grad_bias_out: float32 [768], replicated
- grad_gain_attn: float32 [768], replicated
- grad_shift_attn: float32 [768], replicated
- grad_w_up: float32 [768, 3072], P(None, 'mp')
- grad_bias_up: float32 [3072], P('mp')
- grad_w_down: float32 [3072, 768], P('mp')
- grad_bias_down: float32 [768], replicated
- grad_gain_mlp: float32 [768], replicated
- grad_shift_mlp: float32 [768], replicated
The draws below stay inside these ranges and needn't reach their ends.
Inputs may be any that keep to these rules, and one draw needn't show every extreme that they name: `doc_ids`: within a slot the ids never fall; each of the 8 documents covers 1 to 192 rows, one exactly that many.
All inputs are finite; a program needn't handle non-finite values.
Results may differ from the reference program's by a relative error of at most 0.02.
Values may be sent and summed in bfloat16 or wider, within the bound.
No kernel may reach another device: no remote copies, remote signals or barrier semaphores. Data moves between devices by JAX's collectives and lax.ppermute only.
A program may use at most 128 MiB of HBM per device.

```python
import math
import jax
import jax.numpy as jnp
import numpy as np
from jax import lax

D = 768
HEADS = 12
HEAD_DIM = 64
FF = 3072
SLOT = 512
DOCS = 8
SLOTS_DEV = 4
SLOTS = 32
ROWS = 16384


def draw_out_grad(key, part):
    row_total = ROWS
    first_key = jax.random.fold_in(key, 11)
    ramp = 0.5 + jnp.arange(row_total, dtype=jnp.float32) / max(row_total - 1, 1)
    base = jnp.clip(jax.random.normal(first_key, (row_total, D), jnp.float32), -4.0, 4.0)
    values = base * ramp[:, None]
    return values.astype(jnp.bfloat16)


def levels(own_key, dims, pieces, smallest, top_value):
    factor_of, own = 1.0, jax.random.fold_in(own_key, 6)
    for position, blocks in pieces:
        heights = jnp.exp(jax.random.uniform(jax.random.fold_in(own, position), (blocks,), jnp.float32, smallest / len(pieces), top_value / len(pieces)))
        factor_of = factor_of * jnp.repeat(heights, dims[position] // blocks).reshape([-1 if axis == position else 1 for axis in range(len(dims))])
    return factor_of


def profile(count, total, reach, slope):
    weights = [(1 << 20) // math.isqrt(standing ** slope) + 1 for standing in range(2, count + 1)]
    rest, counts = total - reach - (count - 1), [1] * (count - 1)
    while rest > 0:
        candidates = [i for i in range(count - 1) if counts[i] < reach]
        mass, budget = sum([weights[i] for i in candidates]), rest
        for i in candidates:
            addition = min(reach - counts[i], max(1, budget * weights[i] // mass), rest)
            counts[i] = counts[i] + addition
            rest = rest - addition
    return np.array([reach] + counts)


def uneven(rng, amount, total, limit, lean):
    if amount == 2:
        one = jax.random.randint(rng, (), max(1, total - limit), min(limit, total - 1) + 1)
        return jnp.stack([one, total - one])
    sizes = jnp.asarray(profile(amount, total, limit, lean), jnp.int32)
    twos = (amount - 1) // 2
    donor, sink = sizes[1:1 + 2 * twos:2], sizes[2:2 + 2 * twos:2]
    room = jnp.minimum(donor - 1, limit - sink)
    passed = jax.random.randint(jax.random.fold_in(rng, 1), (twos,), 0, 1 << 20) % (room + 1)
    sizes = sizes.at[1:1 + 2 * twos:2].set(donor - passed).at[2:2 + 2 * twos:2].set(sink + passed)
    return sizes[jax.random.permutation(jax.random.fold_in(rng, 2), amount)]


def normal_values(stream_key, extent, scale, limit, cuts=(), held_as=jnp.bfloat16):
    result = scale * jax.random.normal(stream_key, extent, jnp.float32)
    if cuts:
        result = result * levels(stream_key, extent, cuts, -0.22, 0.18)
    return jnp.clip(result, -limit, limit).astype(held_as)


def setup_inputs(seed: int = 0) -> dict:
    key_of = jax.random.split(jax.random.key(seed), 16)
    return {
        "tokens": normal_values(key_of[0], (ROWS, D), 1.0, 6.0, ((0, 32),)),
        "doc_ids": jax.vmap(lambda own: jnp.searchsorted(jnp.cumsum(uneven(own, DOCS, SLOT, 3 * SLOT // 8, 1)), jnp.arange(SLOT), side="right"))(jax.random.split(key_of[1], SLOTS)).reshape((SLOTS, SLOT)).astype(jnp.int32),
        "w_qkv": normal_values(key_of[2], (3, D, D), D ** -0.5, 0.21875, ((2, 4),)),
        "bias_qv": normal_values(key_of[3], (2, D), 0.5, 3.0, ((1, 4),)),
        "w_out": normal_values(key_of[4], (D, D), (max(1, D * DOCS // SLOT)) ** -0.5, 1.75, ((0, 4),)),
        "bias_out": normal_values(key_of[5], (D,), 0.3, 2.0),
        "gain_attn": jnp.clip(1.0 + 0.1 * jax.random.normal(key_of[6], (D,), jnp.float32), 0.5, 1.5).astype(jnp.bfloat16),
        "shift_attn": normal_values(key_of[7], (D,), 0.3, 2.0),
        "w_up": normal_values(key_of[8], (D, FF), D ** -0.5, 0.21875, ((1, 4),)),
        "bias_up": normal_values(key_of[9], (FF,), 0.5, 3.0, ((0, 4),)),
        "w_down": normal_values(key_of[10], (FF, D), FF ** -0.5, 0.109375, ((0, 4),)),
        "bias_down": normal_values(key_of[11], (D,), 0.3, 2.0),
        "gain_mlp": jnp.clip(1.0 + 0.1 * jax.random.normal(key_of[12], (D,), jnp.float32), 0.5, 1.5).astype(jnp.bfloat16),
        "shift_mlp": normal_values(key_of[13], (D,), 0.3, 2.0),
        "out_grad": draw_out_grad(jax.random.fold_in(key_of[15], 71), 0),
    }


@jax.custom_vjp
def low(v):
    return lax.optimization_barrier(v.astype(jnp.bfloat16)).astype(jnp.float32)

@jax.custom_vjp
def low_back(v):
    return v

def low_keep(v):
    return (low(v), None)

def low_pass(kept, grad):
    return (grad,)

def back_keep(v):
    return (v, None)

def back_low(kept, grad):
    return (low(grad),)
low.defvjp(low_keep, low_pass)
low_back.defvjp(back_keep, back_low)
NORM_EPS = 1e-05
HIGHEST_PREC = lax.Precision.HIGHEST

def layer_norm(rows, gain, shift):
    mean_row = lax.optimization_barrier(jnp.mean(rows, axis=-1, keepdims=True))
    centred = rows - mean_row
    spread = lax.optimization_barrier(jnp.mean(centred * centred, axis=-1, keepdims=True))
    return centred * lax.rsqrt(spread + NORM_EPS) * gain + shift

def slot_attention(inputs):
    triple, slot_ids = inputs
    same_doc = slot_ids[:, None] == slot_ids[None, :]
    scores = jnp.einsum('qhd,khd->hqk', triple[0], triple[1], precision=HIGHEST_PREC) * HEAD_DIM ** (-0.5)
    scores = low_back(scores)
    scores = jnp.where(same_doc[None], scores, -1e+30)
    attn_probs = jax.nn.softmax(scores, axis=-1)
    attended = jnp.einsum('hqk,khd->qhd', low(attn_probs), triple[2], precision=HIGHEST_PREC)
    return attended.reshape(SLOT, HEADS * HEAD_DIM)

def block_layer(tokens, doc_ids, params):
    w_qkv, bias_qv, w_out, bias_out, gain_attn, shift_attn, w_up, bias_up, w_down, bias_down, gain_mlp, shift_mlp = params
    projected = jnp.einsum('rd,tde->tre', tokens, w_qkv, precision=HIGHEST_PREC)
    zero_bias = jnp.zeros_like(bias_qv[0])
    triple = projected + jnp.stack([bias_qv[0], zero_bias, bias_qv[1]])[:, None, :]
    triple = low(low_back(triple))
    slot_count = doc_ids.shape[0]
    per_slot = jnp.moveaxis(triple.reshape(3, slot_count, SLOT, HEADS, HEAD_DIM), 1, 0)
    mixed = lax.map(jax.checkpoint(slot_attention), (per_slot, doc_ids))
    mixed = low(low_back(mixed.reshape(slot_count * SLOT, D)))
    attn_part = low_back(jnp.dot(mixed, w_out, precision=HIGHEST_PREC))
    normed_attn = layer_norm(tokens + attn_part + bias_out, gain_attn, shift_attn)
    pre_act = low_back(jnp.dot(low(normed_attn), w_up, precision=HIGHEST_PREC) + bias_up)
    act_value = low(jax.nn.gelu(pre_act, approximate=False))
    mlp_branch = low_back(jnp.dot(act_value, w_down, precision=HIGHEST_PREC))
    return layer_norm(normed_attn + mlp_branch + bias_down, gain_mlp, shift_mlp)

def reference(tokens, doc_ids, w_qkv, bias_qv, w_out, bias_out, gain_attn, shift_attn, w_up, bias_up, w_down, bias_down, gain_mlp, shift_mlp, out_grad):
    params = tuple((weight_arr.astype(jnp.float32) for weight_arr in (w_qkv, bias_qv, w_out, bias_out, gain_attn, shift_attn, w_up, bias_up, w_down, bias_down, gain_mlp, shift_mlp)))
    group_rows = SLOTS_DEV * SLOT
    groups = SLOTS // SLOTS_DEV
    token_groups = tokens.astype(jnp.float32).reshape(groups, group_rows, D)
    grad_groups = out_grad.astype(jnp.float32).reshape(groups, group_rows, D)
    id_groups = doc_ids.reshape(groups, SLOTS_DEV, SLOT)

    def one_group(totals, inputs):
        rows_in, grad_in, ids_in = inputs

        def forward(rows, params_in):
            return block_layer(rows, ids_in, params_in)
        outputs, pullback = jax.vjp(forward, rows_in, params)
        grad_rows, grad_params = pullback(grad_in)
        totals = jax.tree.map(lambda summed, added: summed + added, totals, grad_params)
        return (totals, (outputs.astype(jnp.bfloat16), grad_rows.astype(jnp.bfloat16)))
    starting = jax.tree.map(jnp.zeros_like, params)
    totals, (outs_all, grads_all) = lax.scan(one_group, starting, (token_groups, grad_groups, id_groups))
    layer_out = outs_all.reshape(ROWS, D)
    grad_tokens = grads_all.reshape(ROWS, D)
    return (layer_out, grad_tokens, totals[0], totals[1], totals[2], totals[3], totals[4], totals[5], totals[6], totals[7], totals[8], totals[9], totals[10], totals[11])
```

```python
import jax
import jax.numpy as jnp
from jax import lax
from jax.sharding import PartitionSpec as P

HEAD_DIM = 64
NORM_EPS = 1e-05
BF = jnp.bfloat16
F32 = jnp.float32

CORE, Y, X, Z1, Z2 = range(5)
STEP = {CORE: ("dp", 1), Y: ("dp", 4), X: ("dp", 2), Z1: ("mp", 1), Z2: ("mp", 2)}


def dot(left, right, dims):
    return lax.dot_general(left, right, (dims, ((), ())), preferred_element_type=F32)


def build(mesh):
    dp_size, mp_size = mesh.shape["dp"], mesh.shape["mp"]
    assert dp_size % 8 == 0 and mp_size == 4 and dp_size & (dp_size - 1) == 0
    extra = []
    bit = 8
    while bit < dp_size:
        extra.append(bit)
        bit *= 2

    def swap(value, axis_name, k):
        size = dp_size if axis_name == "dp" else mp_size
        return lax.ppermute(value, axis_name, [(i, i ^ k) for i in range(size)])

    def grow(cur, axis):
        return lax.concatenate([cur, swap(cur, *STEP[axis])], axis)

    def gather(piece, order):
        for axis in order:
            piece = grow(piece, axis)
        return piece

    def halve(cur, axis):
        keep = lax.slice_in_dim(cur, 0, 1, axis=axis)
        send = lax.slice_in_dim(cur, 1, 2, axis=axis)
        return (keep.astype(F32) + swap(send, *STEP[axis]).astype(F32)).astype(BF)

    def fold(cur, axis_name, k):
        return (cur.astype(F32) + swap(cur, axis_name, k).astype(F32)).astype(BF)

    def scatter(cur, order, whole=()):
        for axis in order:
            cur = fold(cur, *STEP[axis]) if axis in whole else halve(cur, axis)
        for k in extra:
            cur = fold(cur, "dp", k)
        return cur

    def shards(
        tokens, doc_ids, w_qkv, bias_qv, w_out, bias_out, gain_attn, shift_attn,
        w_up, bias_up, w_down, bias_down, gain_mlp, shift_mlp, out_grad,
    ):
        rows, width = tokens.shape
        slot_len = doc_ids.shape[1]
        assert rows == slot_len
        local = w_qkv.shape[2]
        heads_loc = local // HEAD_DIM
        heads = heads_loc * mp_size
        ff_loc = w_up.shape[1]
        unit = ff_loc // 8
        sub = HEAD_DIM // 4
        scale = HEAD_DIM**-0.5
        dp_id, mp_id = lax.axis_index("dp"), lax.axis_index("mp")
        bits = {CORE: dp_id & 1, X: (dp_id >> 1) & 1, Y: (dp_id >> 2) & 1}

        def place(value, at):
            for axis, key in at:
                value = jnp.where(bits[key] == 1, jnp.flip(value, axis), value)
            return value

        def pick(value, at):
            for axis, key in at:
                value = lax.dynamic_slice_in_dim(value, bits[key], 1, axis)
            return value

        qkv_rows = jnp.swapaxes(w_qkv, 1, 2).reshape(3, heads_loc, 2, 2, sub, width)
        out_rows = w_out.reshape(1, heads_loc, 2, 2, sub, width)
        attn_rows = jnp.concatenate([qkv_rows, out_rows], 0)
        attn_piece = pick(attn_rows, ((2, CORE), (3, X))).reshape(1, 1, 1, 1, 1, -1, width)
        up_piece = pick(w_up.T.reshape(2, 2, 2, unit, width), ((0, CORE), (1, Y), (2, X)))
        down_piece = pick(w_down.reshape(2, 2, 2, unit, width), ((0, CORE), (1, Y), (2, X)))
        small = jnp.concatenate([bias_qv.reshape(1, 1, -1), bias_up.reshape(1, 1, -1)], 2)
        small = lax.concatenate([small, swap(small, "mp", 2)], 1)
        small = lax.concatenate([small, swap(small, "mp", 1)], 0)
        attn_w = gather(attn_piece, (Z2, Z1, X, CORE))
        attn_w = attn_w.reshape(2, 2, 2, 2, 4, heads_loc, sub, width)
        attn_w = attn_w.transpose(4, 2, 3, 5, 0, 1, 6, 7).reshape(4, width, width)
        up_w = gather(up_piece.reshape(1, 1, 1, 1, 1, unit, width), (Z2, Z1, X, Y))
        up_w = [up_w.reshape(-1, width), swap(up_w, *STEP[CORE]).reshape(-1, width)]
        down_w = gather(down_piece.reshape(1, 1, 1, 1, 1, unit, width), (Z2, Z1, X, Y))
        down_w = [down_w.reshape(-1, width), swap(down_w, *STEP[CORE]).reshape(-1, width)]

        bias_q, bias_v = (
            place(small[..., i * local : (i + 1) * local].reshape(2, 2, heads_loc, 2, 2, sub), ((3, CORE), (4, X)))
            .reshape(-1, 1)
            .astype(F32)
            for i in range(2)
        )
        bias_u = small[..., 2 * local :].reshape(2, 2, 2, 2, 2, unit)
        bias_u = place(bias_u, ((2, CORE), (3, Y), (4, X))).transpose(2, 3, 4, 0, 1, 5)
        bias_u = bias_u.reshape(2, 1, -1).astype(F32)

        wide = tokens.astype(F32)
        proj = dot(attn_w[:3].reshape(3 * width, width), tokens, ((1,), (1,))).reshape(3, width, rows)
        query = (proj[0] + bias_q).astype(BF).reshape(heads, HEAD_DIM, rows)
        key = proj[1].astype(BF).reshape(heads, HEAD_DIM, rows)
        value = (proj[2] + bias_v).astype(BF).reshape(heads, HEAD_DIM, rows)
        ids = lax.dynamic_slice_in_dim(doc_ids, mp_id, 1, 0)
        same = ids.reshape(rows, 1) == ids.reshape(1, rows)
        scores = jnp.einsum("hdq,hdk->hqk", query, key, preferred_element_type=F32) * scale
        scores = jnp.where(same[None], scores, -1e30)
        top = jnp.max(scores, axis=-1, keepdims=True)
        probs = jnp.exp(scores - top)
        probs = probs / jnp.sum(probs, axis=-1, keepdims=True)
        probs_low = probs.astype(BF)
        mixed = jnp.einsum("hdk,hqk->hdq", value, probs_low, preferred_element_type=F32)
        mixed = mixed.astype(BF).reshape(width, rows)

        def stats(value):
            mean = jnp.mean(value, axis=-1, keepdims=True)
            centred = value - mean
            inv = lax.rsqrt(jnp.mean(centred * centred, axis=-1, keepdims=True) + NORM_EPS)
            return centred * inv, inv

        def norm_back(grad, gain, normed, inv):
            e = grad * gain
            m1 = jnp.mean(e, axis=-1, keepdims=True)
            m2 = jnp.mean(e * normed, axis=-1, keepdims=True)
            return (e - m1 - normed * m2) * inv

        resid = wide + dot(mixed, attn_w[3], ((0,), (0,))) + bias_out.astype(F32)
        norm1, inv1 = stats(resid)
        h1 = norm1 * gain_attn.astype(F32) + shift_attn.astype(F32)
        h1_low = h1.astype(BF)

        act, slope = [], []
        branch = h1 + bias_down.astype(F32)
        for i in range(2):
            pre = dot(h1_low, up_w[i], ((1,), (1,))) + bias_u[i]
            cdf = 0.5 * (1.0 + lax.erf(pre * (2.0**-0.5)))
            act.append((pre * cdf).astype(BF))
            slope.append((cdf + pre * jnp.exp(-0.5 * pre * pre) * 0.3989422804014327))
            branch = branch + dot(act[i], down_w[i], ((1,), (0,)))
        norm2, inv2 = stats(branch)
        layer_out = (norm2 * gain_mlp.astype(F32) + shift_mlp.astype(F32)).astype(BF)

        g = out_grad.astype(F32)
        d_res2 = norm_back(g, gain_mlp.astype(F32), norm2, inv2)
        d_res2_low = d_res2.astype(BF)
        vec_gain_mlp = jnp.sum(g * norm2, axis=0)
        vec_shift_mlp = jnp.sum(g, axis=0)
        vec_bias_down = jnp.sum(d_res2, axis=0)
        g_down = [None, None]
        g_up = [None, None]
        d_pre = [None, None]
        for i in (1, 0):
            g_down[i] = dot(act[i], d_res2_low, ((0,), (0,))).astype(BF)
        for i in (1, 0):
            d_pre[i] = (dot(d_res2_low, down_w[i], ((1,), (1,))) * slope[i]).astype(BF)
            g_up[i] = dot(d_pre[i], h1_low, ((0,), (0,))).astype(BF)
        d_h1 = d_res2 + dot(d_pre[0], up_w[0], ((1,), (0,))) + dot(d_pre[1], up_w[1], ((1,), (0,)))
        vec_bias_up = jnp.stack([jnp.sum(d, axis=0, dtype=F32) for d in d_pre])

        def core_sum(pair):
            got = swap(pair[1], *STEP[CORE])
            return (pair[0].astype(F32) + got.astype(F32)).astype(BF).reshape(1, 2, 2, 2, 2, unit, width)

        r_down = scatter(core_sum(g_down), (X, Y, Z1, Z2))
        r_up = scatter(core_sum(g_up), (Y, X, Z1, Z2))

        d_res1 = norm_back(d_h1, gain_attn.astype(F32), norm1, inv1)
        d_res1_low = d_res1.astype(BF)
        vec_gain_attn = jnp.sum(d_h1 * norm1, axis=0)
        vec_shift_attn = jnp.sum(d_h1, axis=0)
        vec_bias_out = jnp.sum(d_res1, axis=0)
        g_out = dot(mixed, d_res1_low, ((1,), (0,))).astype(BF)
        d_mixed = dot(attn_w[3], d_res1_low, ((1,), (1,))).astype(BF).reshape(heads, HEAD_DIM, rows)

        d_probs = jnp.einsum("hdq,hdk->hqk", d_mixed, value, preferred_element_type=F32)
        inner = jnp.sum(probs * d_probs, axis=-1, keepdims=True)
        d_scores = (probs * (d_probs - inner)).astype(BF)
        d_query = jnp.einsum("hdk,hqk->hdq", key, d_scores, preferred_element_type=F32) * scale
        d_key = jnp.einsum("hdq,hqk->hdk", query, d_scores, preferred_element_type=F32) * scale
        d_value = jnp.einsum("hdq,hqk->hdk", d_mixed, probs_low, preferred_element_type=F32)
        d_proj = jnp.stack([d_query, d_key, d_value]).astype(BF).reshape(3 * width, rows)
        vec_qv = jnp.sum(d_proj.reshape(3, width, rows), axis=-1, dtype=F32)
        g_qkv = dot(d_proj, tokens, ((1,), (0,))).astype(BF).reshape(3, width, width)
        g_attn = jnp.concatenate([g_qkv, g_out[None]], 0)
        g_attn = g_attn.reshape(4, 2, 2, heads_loc, 2, 2, sub, width).transpose(4, 5, 1, 2, 0, 3, 6, 7)
        r_attn = scatter(g_attn.reshape(2, 1, 2, 2, 2, -1, width), (CORE, X, Y, Z1, Z2), whole=(Y,))
        grad_tokens = (d_res1 + dot(d_proj, attn_w[:3].reshape(3 * width, width), ((0,), (0,)))).astype(BF)

        bias_grads = place(vec_bias_up.reshape(2, 2, 2, 2, 2, unit), ((0, CORE), (1, Y), (2, X)))
        bias_grads = bias_grads.transpose(3, 4, 0, 1, 2, 5).reshape(2, 2, -1)
        qv = jnp.stack([vec_qv[0], vec_qv[2]]).reshape(2, 2, 2, heads_loc, 2, 2, sub)
        qv = place(qv, ((4, CORE), (5, X))).transpose(1, 2, 0, 3, 4, 5, 6).reshape(2, 2, -1)
        sharded = jnp.concatenate([bias_grads, qv], 2)
        shared = jnp.stack(
            [vec_bias_out, vec_gain_attn, vec_shift_attn, vec_bias_down, vec_gain_mlp, vec_shift_mlp]
        )
        n_sharded = sharded.size
        flat = jnp.concatenate([sharded.reshape(-1), shared.reshape(-1)]).reshape(-1, 128)
        for k in [1, 2, 4, *extra]:
            flat = flat + swap(flat, "dp", k)
        for k, axis in ((1, 0), (2, 1)):
            got = swap(flat, "mp", k)
            turn = jnp.flip(got.reshape(-1)[:n_sharded].reshape(sharded.shape), axis)
            flat = flat + jnp.concatenate([turn.reshape(-1), got.reshape(-1)[n_sharded:]]).reshape(-1, 128)
        flat = flat.reshape(-1)
        own = flat[:n_sharded].reshape(sharded.shape)[0, 0]
        shared = flat[n_sharded:].reshape(6, width)
        grad_bias_up = own[:ff_loc]
        grad_bias_qv = own[ff_loc:].reshape(2, local)

        r_down = gather(r_down, (Y, X, CORE)).reshape(2, 2, 2, unit, width)
        r_up = gather(r_up, (X, Y, CORE)).reshape(2, 2, 2, unit, width)
        r_attn = gather(r_attn, (X, CORE)).reshape(2, 2, 4, heads_loc, sub, width)
        at = ((0, CORE), (1, Y), (2, X))
        grad_down = place(r_down, at).astype(F32).reshape(ff_loc, width)
        grad_up = place(r_up, at).reshape(ff_loc, width).T.astype(F32)
        r_attn = place(r_attn, ((0, CORE), (1, X))).transpose(2, 3, 0, 1, 4, 5).reshape(4, local, width)
        grad_w_qkv = jnp.swapaxes(r_attn[:3], 1, 2).astype(F32)
        grad_w_out = r_attn[3].astype(F32)
        return (
            layer_out, grad_tokens, grad_w_qkv, grad_bias_qv, grad_w_out,
            shared[0], shared[1], shared[2], grad_up, grad_bias_up, grad_down, shared[3], shared[4], shared[5],
        )

    return shards


def solution(mesh):
    rows, cols, vec = P(("dp", "mp"), None), P(None, "mp"), P()
    in_specs = (
        rows, P("dp", None), P(None, None, "mp"), cols, P("mp", None), vec, vec, vec,
        cols, P("mp"), P("mp", None), vec, vec, vec, rows,
    )
    out_specs = (
        rows, rows, P(None, None, "mp"), cols, P("mp", None), vec, vec, vec,
        cols, P("mp"), P("mp", None), vec, vec, vec,
    )
    return jax.shard_map(build(mesh), mesh=mesh, in_specs=in_specs, out_specs=out_specs, check_vma=False)
```

```python
import jax
import jax.numpy as jnp
from jax import lax
from jax.experimental import pallas as pl
from jax.experimental.pallas import tpu as pltpu
from jax.sharding import PartitionSpec as P


HEAD_DIM = 64
NORM_EPS = 1e-05
BF = jnp.bfloat16
F32 = jnp.float32

CORE, Y, X, Z1, Z2 = range(5)
CHUNK = 128
STEP = {CORE: ("dp", 1), Y: ("dp", 4), X: ("dp", 2), Z1: ("mp", 1), Z2: ("mp", 2)}


def dot(left, right, dims):
    return lax.dot_general(left, right, (dims, ((), ())), preferred_element_type=F32)


def attend_kernel(ids_row, ids_col, query, key, value, mixed, probs):
    keys = key[...]
    scaled = query[...] * jnp.asarray(HEAD_DIM**-0.5, BF)
    row = ids_row[...]
    for start in range(0, keys.shape[1], CHUNK):
        part = slice(start, start + CHUNK)
        scores = dot(scaled[:, part], keys, ((0,), (0,)))
        scores = jnp.where(ids_col[part, :] == row, scores, -1e30)
        weights = jnp.exp(scores - jnp.max(scores, axis=-1, keepdims=True))
        total = jnp.sum(weights, axis=-1, keepdims=True)
        probs[0, part, :] = (weights * (1.0 / total)).astype(BF)
    mixed[...] = dot(value[...], probs[0], ((1,), (1,))).astype(BF)


def attend(proj, ids):
    rows = proj.shape[1]
    heads = proj.shape[0] // (3 * HEAD_DIM)
    part = lambda t: pl.BlockSpec((HEAD_DIM, rows), lambda h: (t * heads + h, 0))
    return pl.pallas_call(
        attend_kernel,
        name="attend",
        grid=(heads,),
        in_specs=[
            pl.BlockSpec((1, rows), lambda h: (0, 0)),
            pl.BlockSpec((rows, 1), lambda h: (0, 0)),
            part(0), part(1), part(2),
        ],
        out_specs=[
            pl.BlockSpec((HEAD_DIM, rows), lambda h: (h, 0)),
            pl.BlockSpec((1, rows, rows), lambda h: (h, 0, 0)),
        ],
        out_shape=[
            jax.ShapeDtypeStruct((heads * HEAD_DIM, rows), BF),
            jax.ShapeDtypeStruct((heads, rows, rows), BF),
        ],
    )(ids.reshape(1, rows), ids.reshape(rows, 1), proj, proj, proj)


def attend_back_kernel(query, key, value, d_mixed, probs, d_proj, d_scores):
    values, grads = value[...], d_mixed[...]
    for start in range(0, values.shape[1], CHUNK):
        part = slice(start, start + CHUNK)
        weights = probs[0, part, :].astype(F32)
        d_probs = dot(grads[:, part], values, ((0,), (0,)))
        inner = jnp.sum(weights * d_probs, axis=-1, keepdims=True)
        d_scores[part, :] = (weights * (d_probs - inner)).astype(BF)
    scale = jnp.asarray(HEAD_DIM**-0.5, BF)
    ds = d_scores[...]
    d_proj[0] = dot(key[...] * scale, ds, ((1,), (1,))).astype(BF)
    d_proj[1] = dot(query[...] * scale, ds, ((1,), (0,))).astype(BF)
    d_proj[2] = dot(grads, probs[0], ((1,), (0,))).astype(BF)


def attend_back(proj, d_mixed, probs, first, count):
    rows = proj.shape[1]
    heads = probs.shape[0]
    part = lambda t: pl.BlockSpec((HEAD_DIM, rows), lambda h: (t * heads + first + h, 0))
    return pl.pallas_call(
        attend_back_kernel,
        name="attend_back",
        grid=(count,),
        in_specs=[
            part(0), part(1), part(2),
            pl.BlockSpec((HEAD_DIM, rows), lambda h: (first + h, 0)),
            pl.BlockSpec((1, rows, rows), lambda h: (first + h, 0, 0)),
        ],
        out_specs=pl.BlockSpec((3, HEAD_DIM, rows), lambda h: (0, h, 0)),
        out_shape=jax.ShapeDtypeStruct((3, count * HEAD_DIM, rows), BF),
        scratch_shapes=[pltpu.VMEM((rows, rows), BF)],
    )(proj, proj, proj, d_mixed, probs)


def build(mesh):
    dp_size, mp_size = mesh.shape["dp"], mesh.shape["mp"]
    assert dp_size % 8 == 0 and mp_size == 4 and dp_size & (dp_size - 1) == 0
    extra = []
    bit = 8
    while bit < dp_size:
        extra.append(bit)
        bit *= 2

    def swap(value, axis_name, k):
        size = dp_size if axis_name == "dp" else mp_size
        return lax.ppermute(value, axis_name, [(i, i ^ k) for i in range(size)])

    def step(value, axis):
        return swap(value, *STEP[axis])

    def gather(piece, order):
        for axis in order:
            piece = lax.concatenate([piece, step(piece, axis)], axis)
        return piece

    def scatter(cur, order):
        for axis in order:
            keep = lax.slice_in_dim(cur, 0, 1, axis=axis)
            send = lax.slice_in_dim(cur, 1, 2, axis=axis)
            cur = (keep.astype(F32) + step(send, axis).astype(F32)).astype(BF)
        for k in extra:
            cur = (cur.astype(F32) + swap(cur, "dp", k).astype(F32)).astype(BF)
        return cur

    def shards(
        tokens, doc_ids, w_qkv, bias_qv, w_out, bias_out, gain_attn, shift_attn,
        w_up, bias_up, w_down, bias_down, gain_mlp, shift_mlp, out_grad,
    ):
        rows, width = tokens.shape
        slot_len = doc_ids.shape[1]
        assert rows == slot_len
        local = w_qkv.shape[2]
        heads_loc = local // HEAD_DIM
        heads = heads_loc * mp_size
        ff_loc = w_up.shape[1]
        unit = ff_loc // 8
        sub = HEAD_DIM // 8
        dp_id, mp_id = lax.axis_index("dp"), lax.axis_index("mp")
        bits = {CORE: dp_id & 1, X: (dp_id >> 1) & 1, Y: (dp_id >> 2) & 1}

        def place(value, at):
            for axis, key in at:
                value = jnp.where(bits[key] == 1, jnp.flip(value, axis), value)
            return value

        def pick(value, at):
            for axis, key in at:
                value = lax.dynamic_slice_in_dim(value, bits[key], 1, axis)
            return value

        qkv_rows = jnp.swapaxes(w_qkv, 1, 2).reshape(3, heads_loc, 2, 2, 2, sub, width)
        out_rows = w_out.reshape(1, heads_loc, 2, 2, 2, sub, width)
        attn_rows = jnp.concatenate([qkv_rows, out_rows], 0)
        attn_piece = pick(attn_rows, ((2, CORE), (3, Y), (4, X))).reshape(2, 1, 1, 1, 1, 1, -1, width)
        up_piece = pick(w_up.T.reshape(2, 2, 2, unit, width), ((0, CORE), (1, Y), (2, X)))
        down_piece = pick(w_down.reshape(2, 2, 2, unit, width), ((0, CORE), (1, Y), (2, X)))
        small = jnp.concatenate([bias_qv.reshape(1, 1, -1), bias_up.reshape(1, 1, -1)], 2)
        small = lax.concatenate([small, swap(small, "mp", 2)], 1)
        small = lax.concatenate([small, swap(small, "mp", 1)], 0)
        pair = [gather(attn_piece[0], (Z2, Z1, X, Y, CORE)), gather(attn_piece[1], (Z2, Z1, Y, X, CORE))]
        pair = [w.reshape(8, 2, 2, 2, heads_loc, sub, width).transpose(3, 1, 2, 4, 0, 5, 6) for w in pair]
        attn_w = jnp.concatenate([w.reshape(2, width, width) for w in pair], 0)
        up_w = gather(up_piece.reshape(1, 1, 1, 1, 1, unit, width), (Z2, Z1, X, Y))
        up_w = [w.reshape(-1, width) for w in (up_w, step(up_w, CORE))]
        down_w = gather(down_piece.reshape(1, 1, 1, 1, 1, unit, width), (Z2, Z1, Y, X))
        down_w = [w.reshape(-1, width) for w in (down_w, step(down_w, CORE))]

        bias_q, bias_v = (
            place(small[..., i * local : (i + 1) * local].reshape(2, 2, heads_loc, 2, 2, 2, sub), ((3, CORE), (4, Y), (5, X)))
            .reshape(-1, 1)
            .astype(F32)
            for i in range(2)
        )
        bias_u = small[..., 2 * local :].reshape(2, 2, 2, 2, 2, unit)
        bias_u = place(bias_u, ((2, CORE), (3, Y), (4, X))).transpose(2, 3, 4, 0, 1, 5)
        bias_u = bias_u.reshape(2, 1, -1).astype(F32)

        wide = tokens.astype(F32)
        bias_three = jnp.concatenate([bias_q, jnp.zeros_like(bias_q), bias_v], 0)
        proj = (dot(attn_w[:3].reshape(3 * width, width), tokens, ((1,), (1,))) + bias_three).astype(BF)
        ids = lax.dynamic_slice_in_dim(doc_ids, mp_id, 1, 0)
        mixed, probs = attend(proj, ids)

        def stats(value):
            mean = jnp.mean(value, axis=-1, keepdims=True)
            centred = value - mean
            inv = lax.rsqrt(jnp.mean(centred * centred, axis=-1, keepdims=True) + NORM_EPS)
            return centred * inv, inv

        def norm_back(grad, gain, normed, inv):
            e = grad * gain
            m1 = jnp.mean(e, axis=-1, keepdims=True)
            m2 = jnp.mean(e * normed, axis=-1, keepdims=True)
            return (e - m1 - normed * m2) * inv

        resid = wide + dot(mixed, attn_w[3], ((0,), (0,))) + bias_out.astype(F32)
        norm1, inv1 = stats(resid)
        h1 = norm1 * gain_attn.astype(F32) + shift_attn.astype(F32)
        h1_low = h1.astype(BF)

        act, slope = [], []
        branch = h1 + bias_down.astype(F32)
        for i in range(2):
            pre = dot(h1_low, up_w[i], ((1,), (1,))) + bias_u[i]
            cdf = 0.5 * (1.0 + lax.erf(pre * (2.0**-0.5)))
            act.append((pre * cdf).astype(BF))
            slope.append((cdf + pre * jnp.exp(-0.5 * pre * pre) * 0.3989422804014327))
            branch = branch + dot(act[i], down_w[i], ((1,), (0,)))
        norm2, inv2 = stats(branch)
        layer_out = (norm2 * gain_mlp.astype(F32) + shift_mlp.astype(F32)).astype(BF)

        g = out_grad.astype(F32)
        d_res2 = norm_back(g, gain_mlp.astype(F32), norm2, inv2)
        d_res2_low = d_res2.astype(BF)
        vec_gain_mlp = jnp.sum(g * norm2, axis=0)
        vec_shift_mlp = jnp.sum(g, axis=0)
        vec_bias_down = jnp.sum(d_res2, axis=0)
        g_down = [None, None]
        g_up = [None, None]
        d_pre = [None, None]
        for i in (1, 0):
            g_down[i] = dot(act[i], d_res2_low, ((0,), (0,))).astype(BF)
        for i in (1, 0):
            d_pre[i] = (dot(d_res2_low, down_w[i], ((1,), (1,))) * slope[i]).astype(BF)
            g_up[i] = dot(d_pre[i], h1_low, ((0,), (0,))).astype(BF)
        d_h1 = d_res2 + dot(d_pre[0], up_w[0], ((1,), (0,))) + dot(d_pre[1], up_w[1], ((1,), (0,)))
        vec_bias_up = jnp.stack([jnp.sum(d, axis=0, dtype=F32) for d in d_pre])

        def core_sum(pair):
            got = step(pair[1], CORE)
            return (pair[0].astype(F32) + got.astype(F32)).astype(BF).reshape(1, 2, 2, 2, 2, unit, width)

        r_down = scatter(core_sum(g_down), (X, Z1, Z2, Y))
        r_up = scatter(core_sum(g_up), (Y, X, Z1, Z2))

        d_res1 = norm_back(d_h1, gain_attn.astype(F32), norm1, inv1)
        d_res1_low = d_res1.astype(BF)
        vec_gain_attn = jnp.sum(d_h1 * norm1, axis=0)
        vec_shift_attn = jnp.sum(d_h1, axis=0)
        vec_bias_out = jnp.sum(d_res1, axis=0)
        g_out = dot(mixed, d_res1_low, ((1,), (0,))).astype(BF)
        d_mixed = dot(attn_w[3], d_res1_low, ((1,), (1,))).astype(BF)
        parts = []
        for i in range(2):
            parts.append(attend_back(proj, d_mixed, probs, i * heads // 2, heads // 2))
        d_proj = jnp.concatenate(parts, 1).reshape(3 * width, rows)
        vec_qv = jnp.sum(d_proj.reshape(3, width, rows), axis=-1, dtype=F32)
        g_qkv = dot(d_proj, tokens, ((1,), (0,))).astype(BF).reshape(3, width, width)
        pair = [g_qkv[:2], jnp.concatenate([g_qkv[2:], g_out[None]], 0)]
        pair = [
            g.reshape(2, 2, 2, heads_loc, 8, sub, width).transpose(4, 1, 2, 0, 3, 5, 6).reshape(2, 2, 2, 2, 2, -1, width)
            for g in pair
        ]
        r_qk = scatter(pair[0], (CORE, X, Y, Z1, Z2))
        r_vo = scatter(pair[1], (CORE, Y, X, Z1, Z2))
        grad_tokens = (d_res1 + dot(d_proj, attn_w[:3].reshape(3 * width, width), ((0,), (0,)))).astype(BF)

        bias_grads = place(vec_bias_up.reshape(2, 2, 2, 2, 2, unit), ((0, CORE), (1, Y), (2, X)))
        bias_grads = bias_grads.transpose(3, 4, 0, 1, 2, 5).reshape(2, 2, -1)
        qv = jnp.stack([vec_qv[0], vec_qv[2]]).reshape(2, 2, 2, heads_loc, 2, 2, 2, sub)
        qv = place(qv, ((4, CORE), (5, Y), (6, X))).transpose(1, 2, 0, 3, 4, 5, 6, 7).reshape(2, 2, -1)
        sharded = jnp.concatenate([bias_grads, qv], 2)
        shared = jnp.stack(
            [vec_bias_out, vec_gain_attn, vec_shift_attn, vec_bias_down, vec_gain_mlp, vec_shift_mlp]
        )
        n_sharded = sharded.size
        flat = jnp.concatenate([sharded.reshape(-1), shared.reshape(-1)]).reshape(-1, 128)
        for k in [1, 2, 4, *extra]:
            flat = flat + swap(flat, "dp", k)
        for k, axis in ((1, 0), (2, 1)):
            got = swap(flat, "mp", k)
            turn = jnp.flip(got.reshape(-1)[:n_sharded].reshape(sharded.shape), axis)
            flat = flat + jnp.concatenate([turn.reshape(-1), got.reshape(-1)[n_sharded:]]).reshape(-1, 128)
        flat = flat.reshape(-1)
        own = flat[:n_sharded].reshape(sharded.shape)[0, 0]
        shared = flat[n_sharded:].reshape(6, width)
        grad_bias_up = own[:ff_loc]
        grad_bias_qv = own[ff_loc:].reshape(2, local)

        at = ((0, CORE), (1, Y), (2, X))
        r_ff = gather(jnp.concatenate([r_up, r_down], 5), (X, Y, CORE)).reshape(2, 2, 2, 2, unit, width)
        r_ff = place(r_ff, at)
        grad_down = r_ff[:, :, :, 1].astype(F32).reshape(ff_loc, width)
        grad_up = r_ff[:, :, :, 0].reshape(ff_loc, width).T.astype(F32)
        r_attn = gather(jnp.concatenate([r_qk, r_vo], 5), (X, Y, CORE))
        r_attn = place(r_attn.reshape(2, 2, 2, 4, heads_loc, sub, width), at).transpose(3, 4, 0, 1, 2, 5, 6)
        r_attn = r_attn.reshape(4, local, width)
        grad_w_qkv = jnp.swapaxes(r_attn[:3], 1, 2).astype(F32)
        grad_w_out = r_attn[3].astype(F32)
        return (
            layer_out, grad_tokens, grad_w_qkv, grad_bias_qv, grad_w_out,
            shared[0], shared[1], shared[2], grad_up, grad_bias_up, grad_down, shared[3], shared[4], shared[5],
        )

    return shards


def solution(mesh):
    rows, cols, vec = P(("dp", "mp"), None), P(None, "mp"), P()
    in_specs = (
        rows, P("dp", None), P(None, None, "mp"), cols, P("mp", None), vec, vec, vec,
        cols, P("mp"), P("mp", None), vec, vec, vec, rows,
    )
    out_specs = (
        rows, rows, P(None, None, "mp"), cols, P("mp", None), vec, vec, vec,
        cols, P("mp"), P("mp", None), vec, vec, vec,
    )
    body = build(mesh)

    return jax.shard_map(body, mesh=mesh, in_specs=in_specs, out_specs=out_specs, check_vma=False)
```
